512 devices in a mesh: rx: 8 (over z_hi, y), ry: 8 (over z_lo), tp: 8 (over x, core).
Axes of the slice: x: 4, y: 4, z: 16 (z_hi: 2, z_lo: 8; z = z_hi * 8 + z_lo), core: 2. Of those that a mesh axis runs over, the one named last changes fastest.
Arguments:
- weight: float32 [8, 8, 192, 4096], P('rx', 'ry', 'tp'), may hold values from -6 to 6
- public: float32 [8, 8, 192, 4096], P('rx', 'ry', 'tp'), may hold values from -6 to 6
- mixture: float32 [8, 8, 192, 4096], P('rx', 'ry', 'tp'), may hold values from -6 to 6
- moment_one: float32 [8, 8, 192, 4096], P('rx', 'ry', 'tp'), may hold values from -0.6 to 0.6
- moment_two: float32 [8, 8, 192, 4096], P('rx', 'ry', 'tp'), may hold values from 0.01 to 1
- stored: bfloat16 [8, 8, 192, 1024], P('rx', 'ry', 'tp'), may hold values from -6 to 6
- out_grad: bfloat16 [8, 8, 1024, 4096], P('rx', 'ry', 'tp'), may hold values from -0.5 to 0.5
Outputs:
- weight_new: float32 [8, 8, 192, 4096], P('rx', 'ry', 'tp')
- public_new: float32 [8, 8, 192, 4096], P('rx', 'ry', 'tp')
- mixture_new: float32 [8, 8, 192, 4096], P('rx', 'ry', 'tp')
- first_new: float32 [8, 8, 192, 4096], P('rx', 'ry', 'tp')
- second_new: float32 [8, 8, 192, 4096], P('rx', 'ry', 'tp')
The draws below stay inside these ranges and needn't reach their ends.
All inputs are finite; a program needn't handle non-finite values.
Results may differ from the reference program's by a relative error of at most 0.0039.
Values may be sent and summed in bfloat16 or wider, within the bound.
A program may use at most 64 MiB of HBM per device.

```python
import math
import jax
import jax.numpy as jnp

D = 4096
TOK = 1024
ROUNDS = 2
ALL_ROWS = 192
RX_REPL = 8
RY_REPL = 8


def steps_of(key, extent, shards, low, largest):
    factor_of = 1.0
    for position, blocks in shards:
        draws = jax.random.uniform(jax.random.fold_in(jax.random.fold_in(key, 6), position), (blocks,), jnp.float32, low / len(shards), largest / len(shards))
        factor_of = factor_of * jnp.repeat(jnp.exp(draws), extent[position] // blocks).reshape((-1,) + (1,) * (len(extent) - 1 - position))
    return factor_of


def centred(key, extent, width, bound, pieces=(), held_as=jnp.bfloat16):
    loudness = steps_of(key, extent, pieces, -0.22, 0.18) if pieces else 1.0
    entries = jax.random.normal(key, extent, jnp.float32) * width * loudness
    return jnp.minimum(jnp.maximum(entries, -bound), bound).astype(held_as)


def setup_inputs(seed: int = 0) -> dict:
    splits = jax.random.split(jax.random.key(seed), 8)
    return {
        "weight": centred(splits[0], (RX_REPL, RY_REPL, ALL_ROWS, D), 1.0, 6.0, ((0, 8), (1, 8), (2, 8)), jnp.float32),
        "public": centred(splits[1], (RX_REPL, RY_REPL, ALL_ROWS, D), 1.0, 6.0, ((0, 8), (1, 8), (2, 8)), jnp.float32),
        "mixture": centred(splits[2], (RX_REPL, RY_REPL, ALL_ROWS, D), 1.0, 6.0, ((0, 8), (1, 8), (2, 8)), jnp.float32),
        "moment_one": centred(splits[3], (RX_REPL, RY_REPL, ALL_ROWS, D), 0.1, 0.6, ((0, 8), (1, 8), (2, 8)), jnp.float32),
        "moment_two": jnp.clip(jnp.exp(math.log(1.0) - 4.6051702 * jax.random.uniform(splits[4], (RX_REPL, RY_REPL, ALL_ROWS, D), jnp.float32) ** steps_of(splits[4], (RX_REPL, RY_REPL, ALL_ROWS, D), ((0, 8), (1, 8), (2, 8)), -0.2, 0.2)), 0.01, 1.0),
        "stored": centred(splits[5], (RX_REPL, RY_REPL, ALL_ROWS, TOK), 1.0, 6.0, ((0, 8), (1, 8), (2, 8))),
        "out_grad": centred(splits[6], (RX_REPL, RY_REPL, TOK, D), 0.0625, 0.5, ((0, 8), (1, 8), (2, 8))),
    }


beta_one = 0.9
beta_two = 0.95
first_fix = 0.9999734386011124
second_fix = 0.994079470779666
learn_rate = 0.02
decay_rate = 0.1
epsilon = 1e-08
step_size = 0.5

def reference(weight, public, mixture, moment_one, moment_two, stored, out_grad):
    gradient = jnp.einsum('abrt,abtd->abrd', stored.astype(jnp.float32), out_grad.astype(jnp.float32))
    first_new = beta_one * moment_one + (1.0 - beta_one) * gradient
    second_new = beta_two * moment_two + (1.0 - beta_two) * gradient * gradient
    adjusted = first_new / first_fix / (jnp.sqrt(second_new / second_fix) + epsilon)
    current = weight - learn_rate * (adjusted + decay_rate * weight)
    public_new = public
    mixture_new = mixture
    for gossip_turn in range(ROUNDS):
        sent = (current - public_new).astype(jnp.bfloat16).astype(jnp.float32)
        beside_all = jnp.roll(sent, 1, 0) + jnp.roll(sent, -1, 0) + jnp.roll(sent, 1, 1) + jnp.roll(sent, -1, 1)
        public_new = public_new + sent
        mixture_new = mixture_new + (sent + beside_all) / 5.0
        current = current + step_size * (mixture_new - public_new)
    return (current, public_new, mixture_new, first_new, second_new)
```

```python
import functools

import jax
import jax.numpy as jnp
from jax import lax
from jax.experimental import pallas as pl
from jax.experimental.pallas import tpu as pltpu
from jax.sharding import PartitionSpec as P

MESH = pl.DeviceIdType.MESH
ROUNDS = 2
CHUNKS = 4

beta_one = 0.9
beta_two = 0.95
first_fix = 0.9999734386011124
second_fix = 0.994079470779666
learn_rate = 0.02
decay_rate = 0.1
epsilon = 1e-08
step_size = 0.5


def kernel(
    weight_in, public_in, mixture_in, one_in, two_in, stored_in, grad_in,
    weight_out, public_out, mixture_out, one_out, two_out,
    current, public, mixture, one, two,
    acts, grads, parts, shares, sent, near,
    load_sem, acts_send, acts_recv, grads_send, grads_recv,
    share_send, share_recv, near_send, near_recv, pass_send,
):
    rx, ry, tp = lax.axis_index("rx"), lax.axis_index("ry"), lax.axis_index("tp")
    nrx, nry, ntp = lax.axis_size("rx"), lax.axis_size("ry"), lax.axis_size("tp")
    chip, core = tp // 2, lax.rem(tp, 2)
    other = 1 - core
    row = lax.rem(rx, 4)
    rows, width = weight_in.shape
    tokens = grad_in.shape[0]
    half = width // 2
    step = half // CHUNKS

    def beside(d):
        return (rx, ry, lax.rem(tp + d, ntp))

    def around(drx, dry):
        return (lax.rem(rx + drx + nrx, nrx), lax.rem(ry + dry + nry, nry), tp)

    own_acts = pltpu.make_async_copy(
        stored_in.at[:, pl.ds(pl.multiple_of(chip * 2 * tokens, 128), 2 * tokens)],
        acts.at[tp], load_sem.at[5])
    own_acts.start()
    own_grad = pltpu.make_async_copy(
        grad_in.at[:, pl.ds(pl.multiple_of(core * half, 128), half)],
        grads.at[pl.ds(pl.multiple_of(core * tokens, 128), tokens)], load_sem.at[6])
    own_grad.start()
    loads = []
    for i, (src, dst) in enumerate(
        ((one_in, one), (two_in, two), (weight_in, current), (public_in, public), (mixture_in, mixture))
    ):
        copy = pltpu.make_async_copy(src, dst, load_sem.at[i])
        copy.start()
        loads.append(copy)

    barrier = pltpu.get_barrier_semaphore()

    def greet(who):
        pl.semaphore_signal(barrier, inc=1, device_id=who, device_id_type=MESH)

    pl.when(row == 0)(lambda: greet(around(-2, 0)))
    pl.when(row == 3)(lambda: greet(around(2, 0)))
    for who in (around(1, 0), around(-1, 0), around(0, 1), around(0, -1)):
        greet(who)
    for d in range(1, ntp):
        greet(beside(d))
    passes = (row == 1) | (row == 2)
    pl.semaphore_wait(barrier, ntp - 1 + 4 + jnp.where(passes, 1, 0))

    act_copies = []
    for d in range(1, ntp):
        to = lax.rem(tp + d, ntp)
        act_copies.append(pltpu.make_async_remote_copy(
            src_ref=stored_in.at[:, pl.ds(pl.multiple_of((to // 2) * 2 * tokens, 128), 2 * tokens)],
            dst_ref=acts.at[tp],
            send_sem=acts_send.at[d], recv_sem=acts_recv.at[d],
            device_id=beside(d), device_id_type=MESH))
        act_copies[-1].start()
    grad_copies = []
    for k in range(CHUNKS):
        grad_copies.append(pltpu.make_async_remote_copy(
            src_ref=grad_in.at[:, pl.ds(pl.multiple_of(other * half + k * step, 128), step)],
            dst_ref=grads.at[pl.ds(pl.multiple_of(core * tokens, 128), tokens), pl.ds(k * step, step)],
            send_sem=grads_send.at[k], recv_sem=grads_recv.at[k],
            device_id=(rx, ry, chip * 2 + other), device_id_type=MESH))
        grad_copies[-1].start()

    own_acts.wait()
    own_grad.wait()
    for copy in act_copies:
        copy.wait_recv()
    gathered = acts[...].astype(jnp.float32).reshape(ntp * rows, 2 * tokens).astype(jnp.bfloat16)

    share_copies = []
    for k in range(CHUNKS):
        grad_copies[k].wait_recv()
        terms = jnp.dot(gathered, grads[:, k * step:(k + 1) * step], preferred_element_type=jnp.float32)
        for j in range(ntp):
            parts[k, j] = terms[j * rows:(j + 1) * rows].astype(jnp.bfloat16)
        copies = []
        for d in (4, 3, 5, 2, 6, 7, 1):
            copies.append(pltpu.make_async_remote_copy(
                src_ref=parts.at[k, lax.rem(tp + d, ntp)],
                dst_ref=shares.at[k, tp],
                send_sem=share_send.at[k, d], recv_sem=share_recv.at[k, d],
                device_id=beside(d), device_id_type=MESH))
            copies[-1].start()
        share_copies.append(copies)

    def piece(k, h):
        return slice(None), slice(h * half + k * step, h * half + (k + 1) * step)

    def hop(turn, k, h, slot, who):
        return pltpu.make_async_remote_copy(
            src_ref=sent.at[turn, k, h], dst_ref=near.at[turn, k, h, slot],
            send_sem=near_send.at[turn, k, h, slot], recv_sem=near_recv.at[turn, k, h, slot],
            device_id=who, device_id_type=MESH)

    targets = (around(1, 0), around(-1, 0), around(0, 1), around(0, -1))

    def each_hop(turn, k, h, act):
        for slot in range(4):
            copy = hop(turn, k, h, slot, targets[slot])
            if h == 1 and slot < 2:
                pl.when(row != (3, 0)[slot])(functools.partial(act, copy))
            else:
                act(copy)

    pair = jnp.where(lax.rem(row, 2) == 0, 1, 0)

    def passing(turn, k, up):
        slot = 1 if up else 0
        return pltpu.make_async_remote_copy(
            src_ref=near.at[turn, k, 1, slot], dst_ref=near.at[turn, k, 1, 1 - slot],
            send_sem=pass_send.at[turn, k], recv_sem=near_recv.at[turn, k, 1, 1 - slot],
            device_id=around(2 if up else -2, 0), device_id_type=MESH)

    def arrive(turn, k, h, slot):
        hop(turn, k, h, slot, targets[0]).wait_recv()

    def pass_on(turn, k):
        arrive(turn, k, 1, pair)
        pl.when(row == 2)(lambda: passing(turn, k, True).start())
        pl.when(row == 1)(lambda: passing(turn, k, False).start())

    def start(copy):
        copy.start()

    for copy in loads:
        copy.wait()

    for k in range(CHUNKS):
        for copy in share_copies[k]:
            copy.wait_recv()
        shares[k, tp] = parts[k, tp]
        for h in range(2):
            at = piece(k, h)
            gradient = shares[k, h].astype(jnp.float32)
            for other_chip in range(1, ntp // 2):
                gradient += shares[k, 2 * other_chip + h].astype(jnp.float32)
            first_new = beta_one * one[at] + (1.0 - beta_one) * gradient
            second_new = beta_two * two[at] + (1.0 - beta_two) * gradient * gradient
            one_out[at] = first_new
            two_out[at] = second_new
            adjusted = first_new / first_fix / (jnp.sqrt(second_new / second_fix) + epsilon)
            weight = current[at]
            now = weight - learn_rate * (adjusted + decay_rate * weight)
            current[at] = now
            sent[0, k, h] = (now - public[at]).astype(jnp.bfloat16)
            each_hop(0, k, h, start)
        if k:
            pass_on(0, k - 1)
    pass_on(0, CHUNKS - 1)

    for turn in range(ROUNDS):
        for k in range(CHUNKS):
            for h in range(2):
                at = piece(k, h)
                if h == 0:
                    for slot in range(4):
                        arrive(turn, k, h, slot)
                else:
                    arrive(turn, k, h, 1 - pair)
                    arrive(turn, k, h, 2)
                    arrive(turn, k, h, 3)
                beside_all = near[turn, k, h, 0].astype(jnp.float32)
                for slot in range(1, 4):
                    beside_all += near[turn, k, h, slot].astype(jnp.float32)
                own = sent[turn, k, h].astype(jnp.float32)
                public_new = public[at] + own
                mixture_new = mixture[at] + (own + beside_all) / 5.0
                now = current[at] + step_size * (mixture_new - public_new)
                if turn == ROUNDS - 1:
                    weight_out[at] = now
                    public_out[at] = public_new
                    mixture_out[at] = mixture_new
                else:
                    current[at] = now
                    public[at] = public_new
                    mixture[at] = mixture_new
                    sent[turn + 1, k, h] = (now - public_new).astype(jnp.bfloat16)
                    each_hop(turn + 1, k, h, start)
            if turn < ROUNDS - 1 and k:
                pass_on(turn + 1, k - 1)
        if turn < ROUNDS - 1:
            pass_on(turn + 1, CHUNKS - 1)

    for copy in act_copies + grad_copies:
        copy.wait_send()
    for copies in share_copies:
        for copy in copies:
            copy.wait_send()
    for turn in range(ROUNDS):
        for k in range(CHUNKS):
            for h in range(2):
                each_hop(turn, k, h, lambda copy: copy.wait_send())
            pl.when(passes)(lambda turn=turn, k=k: passing(turn, k, True).wait_send())


def per_device(weight, public, mixture, moment_one, moment_two, stored, out_grad):
    rows, width = weight.shape[2:]
    tokens = out_grad.shape[2]
    step = width // 2 // CHUNKS
    ntp = lax.axis_size("tp")
    whole = jax.ShapeDtypeStruct((rows, width), jnp.float32)
    held = pltpu.VMEM((rows, width), jnp.float32)
    dma = pltpu.SemaphoreType.DMA
    outs = pl.pallas_call(
        kernel,
        out_shape=[whole] * 5,
        in_specs=[pl.BlockSpec(memory_space=pl.ANY)] * 7,
        out_specs=[pl.BlockSpec(memory_space=pltpu.VMEM)] * 5,
        scratch_shapes=[held] * 5 + [
            pltpu.VMEM((ntp, rows, 2 * tokens), jnp.bfloat16),
            pltpu.VMEM((2 * tokens, width // 2), jnp.bfloat16),
            pltpu.VMEM((CHUNKS, ntp, rows, step), jnp.bfloat16),
            pltpu.VMEM((CHUNKS, ntp, rows, step), jnp.bfloat16),
            pltpu.VMEM((ROUNDS, CHUNKS, 2, rows, step), jnp.bfloat16),
            pltpu.VMEM((ROUNDS, CHUNKS, 2, 4, rows, step), jnp.bfloat16),
            dma((7,)), dma((ntp,)), dma((ntp,)), dma((CHUNKS,)), dma((CHUNKS,)),
            dma((CHUNKS, ntp)), dma((CHUNKS, ntp)),
            dma((ROUNDS, CHUNKS, 2, 4)), dma((ROUNDS, CHUNKS, 2, 4)), dma((ROUNDS, CHUNKS)),
        ],
        name="gossip_step",
        compiler_params=pltpu.CompilerParams(collective_id=0, has_side_effects=True),
    )(*(a[0, 0] for a in (weight, public, mixture, moment_one, moment_two, stored, out_grad)))
    return tuple(o[None, None] for o in outs)


def solution(mesh):
    spec = P("rx", "ry", "tp", None)
    return jax.shard_map(
        per_device, mesh=mesh, in_specs=(spec,) * 7, out_specs=(spec,) * 5, check_vma=False
    )
```

```python
import functools

import jax
import jax.numpy as jnp
from jax import lax
from jax.experimental import pallas as pl
from jax.experimental.pallas import tpu as pltpu
from jax.sharding import PartitionSpec as P

MESH = pl.DeviceIdType.MESH
ROUNDS = 2
CHUNKS = 4
AHEAD = 2
LAG = 2

beta_one = 0.9
beta_two = 0.95
first_fix = 0.9999734386011124
second_fix = 0.994079470779666
learn_rate = 0.02
decay_rate = 0.1
epsilon = 1e-08
step_size = 0.5


def kernel(
    weight_in, public_in, mixture_in, one_in, two_in, stored_in, grad_in,
    weight_out, public_out, mixture_out, one_out, two_out,
    current, public, mixture, one, two,
    acts, grads, parts, shares, sent, near,
    load_sem, acts_send, acts_recv, grads_send, grads_recv,
    share_send, share_recv, near_send, near_recv, pass_send, turn_send, word,
):
    rx, ry, tp = lax.axis_index("rx"), lax.axis_index("ry"), lax.axis_index("tp")
    nrx, nry, ntp = lax.axis_size("rx"), lax.axis_size("ry"), lax.axis_size("tp")
    chip, core = tp // 2, lax.rem(tp, 2)
    other = 1 - core
    row = lax.rem(rx, 4)
    rows, width = weight_in.shape
    tokens = grad_in.shape[0]
    half = width // 2
    step = half // CHUNKS

    def beside(d):
        return (rx, ry, lax.rem(tp + d, ntp))

    def around(drx, dry):
        return (lax.rem(rx + drx + nrx, nrx), lax.rem(ry + dry + nry, nry), tp)

    own_acts = pltpu.make_async_copy(
        stored_in.at[:, pl.ds(pl.multiple_of(chip * 2 * tokens, 128), 2 * tokens)],
        acts.at[tp], load_sem.at[5])
    own_acts.start()
    own_grad = pltpu.make_async_copy(
        grad_in.at[:, pl.ds(pl.multiple_of(core * half, 128), half)],
        grads.at[pl.ds(pl.multiple_of(core * tokens, 128), tokens)], load_sem.at[6])
    own_grad.start()
    loads = []
    for i, (src, dst) in enumerate(
        ((one_in, one), (two_in, two), (weight_in, current), (public_in, public), (mixture_in, mixture))
    ):
        copy = pltpu.make_async_copy(src, dst, load_sem.at[i])
        copy.start()
        loads.append(copy)

    def along(d):
        z = lax.rem(rx // 4 * nry + ry + d + 2 * nry, 2 * nry)
        return (z // nry * 4 + row, lax.rem(z, nry), tp)

    barrier = pltpu.get_barrier_semaphore()
    near_by = [beside(d) for d in range(1, ntp)] + [along(1), along(-1)]
    near_by += [(rx // 4 * 4 + lax.rem(row + d, 4), ry, tp) for d in range(1, 4)]
    for who in near_by:
        pl.semaphore_signal(barrier, inc=1, device_id=who, device_id_type=MESH)
    pl.semaphore_wait(barrier, len(near_by))

    spans = (1, 2, 4, 1)

    def tell(i):
        for who in (along(spans[i]), along(-spans[i])):
            pl.semaphore_signal(word.at[i], inc=1, device_id=who, device_id_type=MESH)

    def hear(i):
        pl.semaphore_wait(word.at[i], 2)

    edge = (ry == 0) | (ry == nry - 1)
    passes = ((row == 1) | (row == 2)) & ~edge
    corner = ((row == 0) | (row == 3)) & edge

    act_copies = []
    for d in range(1, ntp):
        to = lax.rem(tp + d, ntp)
        act_copies.append(pltpu.make_async_remote_copy(
            src_ref=stored_in.at[:, pl.ds(pl.multiple_of((to // 2) * 2 * tokens, 128), 2 * tokens)],
            dst_ref=acts.at[tp],
            send_sem=acts_send.at[d], recv_sem=acts_recv.at[d],
            device_id=beside(d), device_id_type=MESH))
        act_copies[-1].start()
    grad_copies = []
    for k in range(CHUNKS):
        grad_copies.append(pltpu.make_async_remote_copy(
            src_ref=grad_in.at[:, pl.ds(pl.multiple_of(other * half + k * step, 128), step)],
            dst_ref=grads.at[pl.ds(pl.multiple_of(core * tokens, 128), tokens), pl.ds(k * step, step)],
            send_sem=grads_send.at[k], recv_sem=grads_recv.at[k],
            device_id=(rx, ry, chip * 2 + other), device_id_type=MESH))
        grad_copies[-1].start()

    tell(0)
    hear(0)
    tell(1)
    own_acts.wait()
    own_grad.wait()
    for copy in act_copies:
        copy.wait_recv()
    hear(1)
    tell(2)
    gathered = acts[...].astype(jnp.float32).reshape(ntp * rows, 2 * tokens).astype(jnp.bfloat16)

    share_copies = []
    for k in range(CHUNKS):
        grad_copies[k].wait_recv()
        terms = jnp.dot(gathered, grads[:, k * step:(k + 1) * step], preferred_element_type=jnp.float32)
        for j in range(ntp):
            parts[k, j] = terms[j * rows:(j + 1) * rows].astype(jnp.bfloat16)
        copies = []
        for d in (4, 3, 5, 2, 6, 7, 1):
            copies.append(pltpu.make_async_remote_copy(
                src_ref=parts.at[k, lax.rem(tp + d, ntp)],
                dst_ref=shares.at[k, tp],
                send_sem=share_send.at[k, d], recv_sem=share_recv.at[k, d],
                device_id=beside(d), device_id_type=MESH))
            copies[-1].start()
        share_copies.append(copies)

    def piece(k, h):
        return slice(None), slice(h * half + k * step, h * half + (k + 1) * step)

    def hop(turn, k, h, slot, who):
        return pltpu.make_async_remote_copy(
            src_ref=sent.at[turn, k, h], dst_ref=near.at[turn, k, h, slot],
            send_sem=near_send.at[turn, k, h, slot], recv_sem=near_recv.at[turn, k, h, slot],
            device_id=who, device_id_type=MESH)

    targets = (around(1, 0), around(-1, 0), around(0, 1), around(0, -1))

    def each_hop(turn, k, h, act):
        for slot in range(4):
            copy = hop(turn, k, h, slot, targets[slot])
            if slot < 2:
                here = row != (3, 0)[slot]
                pl.when(here if h else here | ~edge)(functools.partial(act, copy))
            else:
                act(copy)

    pair = jnp.where(lax.rem(row, 2) == 0, 1, 0)

    def passing(turn, k, up):
        slot = 1 if up else 0
        return pltpu.make_async_remote_copy(
            src_ref=near.at[turn, k, 1, slot], dst_ref=near.at[turn, k, 1, 1 - slot],
            send_sem=pass_send.at[turn, k], recv_sem=near_recv.at[turn, k, 1, 1 - slot],
            device_id=around(2 if up else -2, 0), device_id_type=MESH)

    def arrive(turn, k, h, slot):
        hop(turn, k, h, slot, targets[0]).wait_recv()

    def pass_on(turn, k):
        arrive(turn, k, 1, pair)
        pl.when(passes & (row == 2))(lambda: passing(turn, k, True).start())
        pl.when(passes & (row == 1))(lambda: passing(turn, k, False).start())

    wrap = jnp.where(ry == 0, 2, 3)
    beyond = jnp.where(row == 3, 0, 1)
    over = (lax.rem(rx + jnp.where(row == 3, 1, nrx - 1), nrx), nry - 1 - ry, tp)

    def turning(turn, k, h):
        return pltpu.make_async_remote_copy(
            src_ref=near.at[turn, k, h, wrap], dst_ref=near.at[turn, k, h, beyond],
            send_sem=turn_send.at[turn, k, h], recv_sem=near_recv.at[turn, k, h, beyond],
            device_id=over, device_id_type=MESH)

    bent = [0] * ROUNDS

    def bend(turn, last):
        while bent[turn] <= min(last, CHUNKS - 1):
            k = bent[turn]
            bent[turn] += 1
            for h in range(2):
                @pl.when(corner)
                def _():
                    arrive(turn, k, h, wrap)
                    turning(turn, k, h).start()

    def start(copy):
        copy.start()

    for copy in loads:
        copy.wait()
    hear(2)
    tell(3)

    for k in range(CHUNKS):
        for copy in share_copies[k]:
            copy.wait_recv()
        shares[k, tp] = parts[k, tp]
        for h in range(2):
            at = piece(k, h)
            gradient = shares[k, h].astype(jnp.float32)
            for other_chip in range(1, ntp // 2):
                gradient += shares[k, 2 * other_chip + h].astype(jnp.float32)
            first_new = beta_one * one[at] + (1.0 - beta_one) * gradient
            second_new = beta_two * two[at] + (1.0 - beta_two) * gradient * gradient
            one_out[at] = first_new
            two_out[at] = second_new
            adjusted = first_new / first_fix / (jnp.sqrt(second_new / second_fix) + epsilon)
            weight = current[at]
            now = weight - learn_rate * (adjusted + decay_rate * weight)
            current[at] = now
            sent[0, k, h] = (now - public[at]).astype(jnp.bfloat16)
            if k == 0 and h == 0:
                hear(3)
            each_hop(0, k, h, start)
        if k:
            pass_on(0, k - 1)
    pass_on(0, CHUNKS - 1)

    for turn in range(ROUNDS):
        for k in range(CHUNKS):
            bend(turn, k + AHEAD - 1)
            for h in range(2):
                at = piece(k, h)
                pl.when(~corner)(functools.partial(arrive, turn, k, h, wrap))
                arrive(turn, k, h, 5 - wrap)
                arrive(turn, k, h, 1 - pair)
                if h == 0:
                    arrive(turn, k, h, pair)
                beside_all = near[turn, k, h, 0].astype(jnp.float32)
                for slot in range(1, 4):
                    beside_all += near[turn, k, h, slot].astype(jnp.float32)
                own = sent[turn, k, h].astype(jnp.float32)
                public_new = public[at] + own
                mixture_new = mixture[at] + (own + beside_all) / 5.0
                now = current[at] + step_size * (mixture_new - public_new)
                if turn == ROUNDS - 1:
                    weight_out[at] = now
                    public_out[at] = public_new
                    mixture_out[at] = mixture_new
                else:
                    current[at] = now
                    public[at] = public_new
                    mixture[at] = mixture_new
                    sent[turn + 1, k, h] = (now - public_new).astype(jnp.bfloat16)
                    each_hop(turn + 1, k, h, start)
            if turn < ROUNDS - 1:
                if k:
                    pass_on(turn + 1, k - 1)
                if k >= LAG:
                    bend(turn + 1, k - LAG)
        if turn < ROUNDS - 1:
            pass_on(turn + 1, CHUNKS - 1)

    for copy in act_copies + grad_copies:
        copy.wait_send()
    for copies in share_copies:
        for copy in copies:
            copy.wait_send()
    for turn in range(ROUNDS):
        for k in range(CHUNKS):
            for h in range(2):
                each_hop(turn, k, h, lambda copy: copy.wait_send())
                pl.when(corner)(lambda turn=turn, k=k, h=h: turning(turn, k, h).wait_send())
            pl.when(passes)(lambda turn=turn, k=k: passing(turn, k, True).wait_send())


def store(*refs):
    srcs, dsts, sems = refs[:5], refs[5:10], refs[10]
    copies = [pltpu.make_async_copy(src, dst, sems.at[i]) for i, (src, dst) in enumerate(zip(srcs, dsts))]
    for copy in copies:
        copy.start()
    for copy in copies:
        copy.wait()


def per_device(weight, public, mixture, moment_one, moment_two, stored, out_grad):
    rows, width = weight.shape[2:]
    tokens = out_grad.shape[2]
    step = width // 2 // CHUNKS
    ntp = lax.axis_size("tp")
    whole = jax.ShapeDtypeStruct((rows, width), jnp.float32)
    held = pltpu.VMEM((rows, width), jnp.float32)
    dma = pltpu.SemaphoreType.DMA
    outs = pl.pallas_call(
        kernel,
        out_shape=[pltpu.VMEM((rows, width), jnp.float32)] * 5,
        in_specs=[pl.BlockSpec(memory_space=pl.ANY)] * 7,
        out_specs=[pl.BlockSpec(memory_space=pltpu.VMEM)] * 5,
        scratch_shapes=[held] * 5 + [
            pltpu.VMEM((ntp, rows, 2 * tokens), jnp.bfloat16),
            pltpu.VMEM((2 * tokens, width // 2), jnp.bfloat16),
            pltpu.VMEM((CHUNKS, ntp, rows, step), jnp.bfloat16),
            pltpu.VMEM((CHUNKS, ntp, rows, step), jnp.bfloat16),
            pltpu.VMEM((ROUNDS, CHUNKS, 2, rows, step), jnp.bfloat16),
            pltpu.VMEM((ROUNDS, CHUNKS, 2, 4, rows, step), jnp.bfloat16),
            dma((7,)), dma((ntp,)), dma((ntp,)), dma((CHUNKS,)), dma((CHUNKS,)),
            dma((CHUNKS, ntp)), dma((CHUNKS, ntp)),
            dma((ROUNDS, CHUNKS, 2, 4)), dma((ROUNDS, CHUNKS, 2, 4)), dma((ROUNDS, CHUNKS)), dma((ROUNDS, CHUNKS, 2)),
            pltpu.SemaphoreType.REGULAR((4,)),
        ],
        name="gossip_step",
        compiler_params=pltpu.CompilerParams(collective_id=0, has_side_effects=True),
    )(*(a[0, 0] for a in (weight, public, mixture, moment_one, moment_two, stored, out_grad)))
    outs = pl.pallas_call(
        store,
        out_shape=[whole] * 5,
        in_specs=[pl.BlockSpec(memory_space=pltpu.VMEM)] * 5,
        out_specs=[pl.BlockSpec(memory_space=pl.ANY)] * 5,
        scratch_shapes=[dma((5,))],
        name="store",
    )(*(pltpu.with_memory_space_constraint(o, pltpu.VMEM) for o in outs))
    return tuple(o[None, None] for o in outs)


def solution(mesh):
    spec = P("rx", "ry", "tp", None)
    return jax.shard_map(
        per_device, mesh=mesh, in_specs=(spec,) * 7, out_specs=(spec,) * 5, check_vma=False
    )
```

```python
import functools

import jax
import jax.numpy as jnp
from jax import lax
from jax.experimental import pallas as pl
from jax.experimental.pallas import tpu as pltpu
from jax.sharding import PartitionSpec as P

MESH = pl.DeviceIdType.MESH
ROUNDS = 2
WIDTHS = (256, 512, 640, 640)
CHUNKS = len(WIDTHS)
LATE = (0, 2)
AHEAD = ((2, 2), (2, 4))
LAG = 2

beta_one = 0.9
beta_two = 0.95
first_fix = 0.9999734386011124
second_fix = 0.994079470779666
learn_rate = 0.02
decay_rate = 0.1
epsilon = 1e-08
step_size = 0.5


def kernel(
    weight_in, public_in, mixture_in, one_in, two_in, stored_in, grad_in,
    weight_out, public_out, mixture_out, one_out, two_out,
    current, public, mixture, one, two,
    acts, grads, parts, shares, sent, near,
    load_sem, acts_send, acts_recv, grads_send, grads_recv,
    share_send, share_recv, near_send, near_recv, pass_send, turn_send, word,
):
    rx, ry, tp = lax.axis_index("rx"), lax.axis_index("ry"), lax.axis_index("tp")
    nrx, nry, ntp = lax.axis_size("rx"), lax.axis_size("ry"), lax.axis_size("tp")
    chip, core = tp // 2, lax.rem(tp, 2)
    other = 1 - core
    row = lax.rem(rx, 4)
    rows, width = weight_in.shape
    tokens = grad_in.shape[0]
    half = width // 2
    begin = [sum(WIDTHS[:k]) for k in range(CHUNKS)]

    def cut(k):
        return slice(None), pl.ds(0, WIDTHS[k])

    def beside(d):
        return (rx, ry, lax.rem(tp + d, ntp))

    def around(drx, dry):
        return (lax.rem(rx + drx + nrx, nrx), lax.rem(ry + dry + nry, nry), tp)

    own_acts = pltpu.make_async_copy(
        stored_in.at[:, pl.ds(pl.multiple_of(chip * 2 * tokens, 128), 2 * tokens)],
        acts.at[tp], load_sem.at[5])
    own_acts.start()
    own_grad = pltpu.make_async_copy(
        grad_in.at[:, pl.ds(pl.multiple_of(core * half, 128), half)],
        grads.at[pl.ds(pl.multiple_of(core * tokens, 128), tokens)], load_sem.at[6])
    own_grad.start()
    def along(d):
        z = lax.rem(rx // 4 * nry + ry + d + 2 * nry, 2 * nry)
        return (z // nry * 4 + row, lax.rem(z, nry), tp)

    barrier = pltpu.get_barrier_semaphore()
    near_by = [beside(d) for d in range(1, ntp)] + [along(1), along(-1)]
    near_by += [(rx // 4 * 4 + lax.rem(row + d, 4), ry, tp) for d in range(1, 4)]
    for who in near_by:
        pl.semaphore_signal(barrier, inc=1, device_id=who, device_id_type=MESH)
    pl.semaphore_wait(barrier, len(near_by))

    spans = (1, 2, 4, 1)

    def tell(i):
        for who in (along(spans[i]), along(-spans[i])):
            pl.semaphore_signal(word.at[i], inc=1, device_id=who, device_id_type=MESH)

    def hear(i):
        pl.semaphore_wait(word.at[i], 2)

    edge = (ry == 0) | (ry == nry - 1)
    passes = ((row == 1) | (row == 2)) & ~edge
    corner = ((row == 0) | (row == 3)) & edge

    act_copies = []
    for d in range(1, ntp):
        to = lax.rem(tp + d, ntp)
        act_copies.append(pltpu.make_async_remote_copy(
            src_ref=stored_in.at[:, pl.ds(pl.multiple_of((to // 2) * 2 * tokens, 128), 2 * tokens)],
            dst_ref=acts.at[tp],
            send_sem=acts_send.at[d], recv_sem=acts_recv.at[d],
            device_id=beside(d), device_id_type=MESH))
        act_copies[-1].start()
    grad_copies = []
    for k in range(CHUNKS):
        grad_copies.append(pltpu.make_async_remote_copy(
            src_ref=grad_in.at[:, pl.ds(pl.multiple_of(other * half + begin[k], 128), WIDTHS[k])],
            dst_ref=grads.at[pl.ds(pl.multiple_of(core * tokens, 128), tokens), pl.ds(begin[k], WIDTHS[k])],
            send_sem=grads_send.at[k], recv_sem=grads_recv.at[k],
            device_id=(rx, ry, chip * 2 + other), device_id_type=MESH))
        grad_copies[-1].start()

    tell(0)
    loads = []
    for i, (src, dst) in enumerate(
        ((one_in, one), (two_in, two), (weight_in, current), (public_in, public), (mixture_in, mixture))
    ):
        copy = pltpu.make_async_copy(src, dst, load_sem.at[i])
        copy.start()
        loads.append(copy)

    hear(0)
    tell(1)
    own_acts.wait()
    own_grad.wait()
    for copy in act_copies:
        copy.wait_recv()
    hear(1)
    tell(2)
    gathered = acts[...].astype(jnp.float32).reshape(ntp * rows, 2 * tokens).astype(jnp.bfloat16)

    share_copies = []
    for k in range(CHUNKS):
        grad_copies[k].wait_recv()
        terms = jnp.dot(gathered, grads[:, begin[k]:begin[k] + WIDTHS[k]], preferred_element_type=jnp.float32)
        for j in range(ntp):
            parts[(k, j) + cut(k)] = terms[j * rows:(j + 1) * rows].astype(jnp.bfloat16)
        copies = []
        for d in (4, 3, 5, 2, 6, 7, 1):
            copies.append(pltpu.make_async_remote_copy(
                src_ref=parts.at[(k, lax.rem(tp + d, ntp)) + cut(k)],
                dst_ref=shares.at[(k, tp) + cut(k)],
                send_sem=share_send.at[k, d], recv_sem=share_recv.at[k, d],
                device_id=beside(d), device_id_type=MESH))
            copies[-1].start()
        share_copies.append(copies)

    def piece(k, h):
        return slice(None), slice(h * half + begin[k], h * half + begin[k] + WIDTHS[k])

    def hop(turn, k, h, slot, who):
        return pltpu.make_async_remote_copy(
            src_ref=sent.at[(turn, k, h) + cut(k)], dst_ref=near.at[(turn, k, h, slot) + cut(k)],
            send_sem=near_send.at[turn, k, h, slot], recv_sem=near_recv.at[turn, k, h, slot],
            device_id=who, device_id_type=MESH)

    targets = (around(1, 0), around(-1, 0), around(0, 1), around(0, -1))

    early = rx < nrx // 2

    def each_far(turn, k, act):
        for slot in range(2):
            copy = hop(turn, k, 0, slot, targets[slot])
            pl.when(early & (row == (3, 0)[slot]) & ~edge)(functools.partial(act, copy))

    def each_hop(turn, k, h, act):
        for slot in range(4):
            copy = hop(turn, k, h, slot, targets[slot])
            if slot < 2:
                here = row != (3, 0)[slot]
                far = ~edge & ~early if turn else ~edge
                pl.when(here if h else here | far)(functools.partial(act, copy))
            else:
                pl.when(ry == (nry - 1, 0)[slot - 2])(functools.partial(act, copy))

    def each_step(turn, k, act, some=None):
        for h in range(2):
            for slot in range(2, 4):
                copy = hop(turn, k, h, slot, targets[slot])
                here = ry != (nry - 1, 0)[slot - 2]
                pl.when(here if some is None else here & some)(functools.partial(act, copy))

    pair = jnp.where(lax.rem(row, 2) == 0, 1, 0)

    def passing(turn, k, up):
        slot = 1 if up else 0
        return pltpu.make_async_remote_copy(
            src_ref=near.at[(turn, k, 1, slot) + cut(k)], dst_ref=near.at[(turn, k, 1, 1 - slot) + cut(k)],
            send_sem=pass_send.at[turn, k], recv_sem=near_recv.at[turn, k, 1, 1 - slot],
            device_id=around(2 if up else -2, 0), device_id_type=MESH)

    def arrive(turn, k, h, slot):
        hop(turn, k, h, slot, targets[0]).wait_recv()

    def pass_on(turn, k):
        arrive(turn, k, 1, pair)
        now = ~early if turn else True
        pl.when(passes & (row == 2) & now)(lambda: passing(turn, k, True).start())
        pl.when(passes & (row == 1) & now)(lambda: passing(turn, k, False).start())

    def pass_late(turn, k):
        pl.when(passes & (row == 2) & early)(lambda: passing(turn, k, True).start())
        pl.when(passes & (row == 1) & early)(lambda: passing(turn, k, False).start())

    wrap = jnp.where(ry == 0, 2, 3)
    beyond = jnp.where(row == 3, 0, 1)
    over = (lax.rem(rx + jnp.where(row == 3, 1, nrx - 1), nrx), nry - 1 - ry, tp)

    def turning(turn, k, h):
        return pltpu.make_async_remote_copy(
            src_ref=near.at[(turn, k, h, wrap) + cut(k)], dst_ref=near.at[(turn, k, h, beyond) + cut(k)],
            send_sem=turn_send.at[turn, k, h], recv_sem=near_recv.at[turn, k, h, beyond],
            device_id=over, device_id_type=MESH)

    bent = {}

    def bend(turn, last, who):
        here = corner & early if who else corner & ~early
        while bent.setdefault((turn, who), 0) <= min(last, CHUNKS - 1):
            k = bent[turn, who]
            bent[turn, who] += 1
            for h in range(2):
                @pl.when(here)
                def _():
                    arrive(turn, k, h, wrap)
                    turning(turn, k, h).start()

    def start(copy):
        copy.start()

    hear(2)
    tell(3)
    for copy in loads:
        copy.wait()

    for k in range(CHUNKS):
        for copy in share_copies[k]:
            copy.wait_recv()
        shares[(k, tp) + cut(k)] = parts[(k, tp) + cut(k)]
        for h in range(2):
            at = piece(k, h)
            gradient = shares[(k, h) + cut(k)].astype(jnp.float32)
            for other_chip in range(1, ntp // 2):
                gradient += shares[(k, 2 * other_chip + h) + cut(k)].astype(jnp.float32)
            first_new = beta_one * one[at] + (1.0 - beta_one) * gradient
            second_new = beta_two * two[at] + (1.0 - beta_two) * gradient * gradient
            one_out[at] = first_new
            two_out[at] = second_new
            adjusted = first_new / first_fix / (jnp.sqrt(second_new / second_fix) + epsilon)
            weight = current[at]
            now = weight - learn_rate * (adjusted + decay_rate * weight)
            current[at] = now
            sent[(0, k, h) + cut(k)] = (now - public[at]).astype(jnp.bfloat16)
            if k == 0 and h == 0:
                hear(3)
            each_hop(0, k, h, start)
        if k:
            pass_on(0, k - 1)
        if k >= LATE[0]:
            each_step(0, k - LATE[0], start)
    for k in range(CHUNKS - LATE[0], CHUNKS):
        each_step(0, k, start)
    pass_on(0, CHUNKS - 1)

    for turn in range(ROUNDS):
        for k in range(CHUNKS):
            bend(turn, k + AHEAD[turn][0] - 1, True)
            bend(turn, k + AHEAD[turn][1] - 1, False)
            for h in range(2):
                at = piece(k, h)
                pl.when(~corner)(functools.partial(arrive, turn, k, h, wrap))
                arrive(turn, k, h, 5 - wrap)
                arrive(turn, k, h, 1 - pair)
                if h == 0:
                    arrive(turn, k, h, pair)
                beside_all = near[(turn, k, h, 0) + cut(k)].astype(jnp.float32)
                for slot in range(1, 4):
                    beside_all += near[(turn, k, h, slot) + cut(k)].astype(jnp.float32)
                own = sent[(turn, k, h) + cut(k)].astype(jnp.float32)
                public_new = public[at] + own
                mixture_new = mixture[at] + (own + beside_all) / 5.0
                now = current[at] + step_size * (mixture_new - public_new)
                if turn == ROUNDS - 1:
                    weight_out[at] = now
                    public_out[at] = public_new
                    mixture_out[at] = mixture_new
                else:
                    current[at] = now
                    public[at] = public_new
                    mixture[at] = mixture_new
                    sent[(turn + 1, k, h) + cut(k)] = (now - public_new).astype(jnp.bfloat16)
                    each_hop(turn + 1, k, h, start)
            if turn < ROUNDS - 1:
                if k:
                    pass_on(turn + 1, k - 1)
                if k >= LAG:
                    bend(turn + 1, k - LAG, True)
                    bend(turn + 1, k - LAG, False)
                each_step(turn + 1, k, start, early)
        if turn < ROUNDS - 1:
            pass_on(turn + 1, CHUNKS - 1)
            for k in range(CHUNKS):
                each_step(turn + 1, k, start, ~early)
                each_far(turn + 1, k, start)
                pass_late(turn + 1, k)

    for copy in act_copies + grad_copies:
        copy.wait_send()
    for copies in share_copies:
        for copy in copies:
            copy.wait_send()
    for turn in range(ROUNDS):
        for k in range(CHUNKS):
            each_step(turn, k, lambda copy: copy.wait_send())
            if turn:
                each_far(turn, k, lambda copy: copy.wait_send())
            for h in range(2):
                each_hop(turn, k, h, lambda copy: copy.wait_send())
                pl.when(corner)(lambda turn=turn, k=k, h=h: turning(turn, k, h).wait_send())
            pl.when(passes)(lambda turn=turn, k=k: passing(turn, k, True).wait_send())


def store(*refs):
    srcs, dsts, sems = refs[:5], refs[5:10], refs[10]
    copies = [pltpu.make_async_copy(src, dst, sems.at[i]) for i, (src, dst) in enumerate(zip(srcs, dsts))]
    for copy in copies:
        copy.start()
    for copy in copies:
        copy.wait()


def per_device(weight, public, mixture, moment_one, moment_two, stored, out_grad):
    rows, width = weight.shape[2:]
    tokens = out_grad.shape[2]
    step = max(WIDTHS)
    assert 2 * sum(WIDTHS) == width
    ntp = lax.axis_size("tp")
    whole = jax.ShapeDtypeStruct((rows, width), jnp.float32)
    held = pltpu.VMEM((rows, width), jnp.float32)
    dma = pltpu.SemaphoreType.DMA
    outs = pl.pallas_call(
        kernel,
        out_shape=[pltpu.VMEM((rows, width), jnp.float32)] * 5,
        in_specs=[pl.BlockSpec(memory_space=pl.ANY)] * 7,
        out_specs=[pl.BlockSpec(memory_space=pltpu.VMEM)] * 5,
        scratch_shapes=[held] * 5 + [
            pltpu.VMEM((ntp, rows, 2 * tokens), jnp.bfloat16),
            pltpu.VMEM((2 * tokens, width // 2), jnp.bfloat16),
            pltpu.VMEM((CHUNKS, ntp, rows, step), jnp.bfloat16),
            pltpu.VMEM((CHUNKS, ntp, rows, step), jnp.bfloat16),
            pltpu.VMEM((ROUNDS, CHUNKS, 2, rows, step), jnp.bfloat16),
            pltpu.VMEM((ROUNDS, CHUNKS, 2, 4, rows, step), jnp.bfloat16),
            dma((7,)), dma((ntp,)), dma((ntp,)), dma((CHUNKS,)), dma((CHUNKS,)),
            dma((CHUNKS, ntp)), dma((CHUNKS, ntp)),
            dma((ROUNDS, CHUNKS, 2, 4)), dma((ROUNDS, CHUNKS, 2, 4)), dma((ROUNDS, CHUNKS)), dma((ROUNDS, CHUNKS, 2)),
            pltpu.SemaphoreType.REGULAR((4,)),
        ],
        name="gossip_step",
        compiler_params=pltpu.CompilerParams(collective_id=0, has_side_effects=True),
    )(*(a[0, 0] for a in (weight, public, mixture, moment_one, moment_two, stored, out_grad)))
    outs = pl.pallas_call(
        store,
        out_shape=[whole] * 5,
        in_specs=[pl.BlockSpec(memory_space=pltpu.VMEM)] * 5,
        out_specs=[pl.BlockSpec(memory_space=pl.ANY)] * 5,
        scratch_shapes=[dma((5,))],
        name="store",
    )(*(pltpu.with_memory_space_constraint(o, pltpu.VMEM) for o in outs))
    return tuple(o[None, None] for o in outs)


def solution(mesh):
    spec = P("rx", "ry", "tp", None)
    return jax.shard_map(
        per_device, mesh=mesh, in_specs=(spec,) * 7, out_specs=(spec,) * 5, check_vma=False
    )
```

```python
import functools

import jax
import jax.numpy as jnp
from jax import lax
from jax.experimental import pallas as pl
from jax.experimental.pallas import tpu as pltpu
from jax.sharding import PartitionSpec as P

MESH = pl.DeviceIdType.MESH
ROUNDS = 2
WIDTHS = (256, 512, 640, 640)
CHUNKS = len(WIDTHS)
AHEAD = ((2, 2), (2, 4))
LAG = 2

beta_one = 0.9
beta_two = 0.95
first_fix = 0.9999734386011124
second_fix = 0.994079470779666
learn_rate = 0.02
decay_rate = 0.1
epsilon = 1e-08
step_size = 0.5


def kernel(
    weight_in, public_in, mixture_in, one_in, two_in, stored_in, grad_in,
    weight_out, public_out, mixture_out, one_out, two_out,
    current, public, mixture, one, two,
    acts, grads, parts, shares, sent, near,
    load_sem, acts_send, acts_recv, grads_send, grads_recv,
    share_send, share_recv, near_send, near_recv, pass_send, turn_send, word,
):
    rx, ry, tp = lax.axis_index("rx"), lax.axis_index("ry"), lax.axis_index("tp")
    nrx, nry, ntp = lax.axis_size("rx"), lax.axis_size("ry"), lax.axis_size("tp")
    chip, core = tp // 2, lax.rem(tp, 2)
    other = 1 - core
    row = lax.rem(rx, 4)
    rows, width = weight_in.shape
    tokens = grad_in.shape[0]
    half = width // 2
    begin = [sum(WIDTHS[:k]) for k in range(CHUNKS)]

    def cut(k):
        return slice(None), pl.ds(0, WIDTHS[k])

    def beside(d):
        return (rx, ry, lax.rem(tp + d, ntp))

    def around(drx, dry):
        return (lax.rem(rx + drx + nrx, nrx), lax.rem(ry + dry + nry, nry), tp)

    own_acts = pltpu.make_async_copy(
        stored_in.at[:, pl.ds(pl.multiple_of(chip * 2 * tokens, 128), 2 * tokens)],
        acts.at[tp], load_sem.at[5])
    own_acts.start()
    own_grad = pltpu.make_async_copy(
        grad_in.at[:, pl.ds(pl.multiple_of(core * half, 128), half)],
        grads.at[pl.ds(pl.multiple_of(core * tokens, 128), tokens)], load_sem.at[6])
    own_grad.start()
    def along(d):
        z = lax.rem(rx // 4 * nry + ry + d + 2 * nry, 2 * nry)
        return (z // nry * 4 + row, lax.rem(z, nry), tp)

    barrier = pltpu.get_barrier_semaphore()
    near_by = [beside(d) for d in range(1, ntp)] + [along(1), along(-1)]
    near_by += [(rx // 4 * 4 + lax.rem(row + d, 4), ry, tp) for d in range(1, 4)]
    for who in near_by:
        pl.semaphore_signal(barrier, inc=1, device_id=who, device_id_type=MESH)
    pl.semaphore_wait(barrier, len(near_by))

    spans = (1, 2, 4, 1)

    def tell(i):
        for who in (along(spans[i]), along(-spans[i])):
            pl.semaphore_signal(word.at[i], inc=1, device_id=who, device_id_type=MESH)

    def hear(i):
        pl.semaphore_wait(word.at[i], 2)

    edge = (ry == 0) | (ry == nry - 1)
    passes = ((row == 1) | (row == 2)) & ~edge
    corner = ((row == 0) | (row == 3)) & edge

    act_copies = []
    for d in range(1, ntp):
        to = lax.rem(tp + d, ntp)
        act_copies.append(pltpu.make_async_remote_copy(
            src_ref=stored_in.at[:, pl.ds(pl.multiple_of((to // 2) * 2 * tokens, 128), 2 * tokens)],
            dst_ref=acts.at[tp],
            send_sem=acts_send.at[d], recv_sem=acts_recv.at[d],
            device_id=beside(d), device_id_type=MESH))
        act_copies[-1].start()
    grad_copies = []
    for k in range(CHUNKS):
        grad_copies.append(pltpu.make_async_remote_copy(
            src_ref=grad_in.at[:, pl.ds(pl.multiple_of(other * half + begin[k], 128), WIDTHS[k])],
            dst_ref=grads.at[pl.ds(pl.multiple_of(core * tokens, 128), tokens), pl.ds(begin[k], WIDTHS[k])],
            send_sem=grads_send.at[k], recv_sem=grads_recv.at[k],
            device_id=(rx, ry, chip * 2 + other), device_id_type=MESH))
        grad_copies[-1].start()

    tell(0)
    loads = []
    for i, (src, dst) in enumerate(
        ((one_in, one), (two_in, two), (weight_in, current), (public_in, public), (mixture_in, mixture))
    ):
        copy = pltpu.make_async_copy(src, dst, load_sem.at[i])
        copy.start()
        loads.append(copy)

    hear(0)
    tell(1)
    own_acts.wait()
    own_grad.wait()
    for copy in act_copies:
        copy.wait_recv()
    hear(1)
    tell(2)
    gathered = acts[...].astype(jnp.float32).reshape(ntp * rows, 2 * tokens).astype(jnp.bfloat16)

    share_copies = []
    for k in range(CHUNKS):
        grad_copies[k].wait_recv()
        terms = jnp.dot(gathered, grads[:, begin[k]:begin[k] + WIDTHS[k]], preferred_element_type=jnp.float32)
        for j in range(ntp):
            parts[(k, j) + cut(k)] = terms[j * rows:(j + 1) * rows].astype(jnp.bfloat16)
        copies = []
        for d in (4, 3, 5, 2, 6, 7, 1):
            copies.append(pltpu.make_async_remote_copy(
                src_ref=parts.at[(k, lax.rem(tp + d, ntp)) + cut(k)],
                dst_ref=shares.at[(k, tp) + cut(k)],
                send_sem=share_send.at[k, d], recv_sem=share_recv.at[k, d],
                device_id=beside(d), device_id_type=MESH))
            copies[-1].start()
        share_copies.append(copies)

    def piece(k, h):
        return slice(None), slice(h * half + begin[k], h * half + begin[k] + WIDTHS[k])

    def hop(turn, k, h, slot, who):
        return pltpu.make_async_remote_copy(
            src_ref=sent.at[(turn, k, h) + cut(k)], dst_ref=near.at[(turn, k, h, slot) + cut(k)],
            send_sem=near_send.at[turn, k, h, slot], recv_sem=near_recv.at[turn, k, h, slot],
            device_id=who, device_id_type=MESH)

    targets = (around(1, 0), around(-1, 0), around(0, 1), around(0, -1))

    early = rx < nrx // 2

    def each_far(turn, k, act):
        for slot in range(2):
            copy = hop(turn, k, 0, slot, targets[slot])
            pl.when(early & (row == (3, 0)[slot]) & ~edge)(functools.partial(act, copy))

    def each_hop(turn, k, h, act):
        for slot in range(4):
            copy = hop(turn, k, h, slot, targets[slot])
            if slot < 2:
                here = row != (3, 0)[slot]
                far = ~edge & ~early if turn else ~edge
                pl.when(here if h else here | far)(functools.partial(act, copy))
            else:
                pl.when(ry == (nry - 1, 0)[slot - 2])(functools.partial(act, copy))

    def each_step(turn, k, act, some=None):
        for h in range(2):
            for slot in range(2, 4):
                copy = hop(turn, k, h, slot, targets[slot])
                here = ry != (nry - 1, 0)[slot - 2]
                pl.when(here if some is None else here & some)(functools.partial(act, copy))

    pair = jnp.where(lax.rem(row, 2) == 0, 1, 0)

    def passing(turn, k, up):
        slot = 1 if up else 0
        return pltpu.make_async_remote_copy(
            src_ref=near.at[(turn, k, 1, slot) + cut(k)], dst_ref=near.at[(turn, k, 1, 1 - slot) + cut(k)],
            send_sem=pass_send.at[turn, k], recv_sem=near_recv.at[turn, k, 1, 1 - slot],
            device_id=around(2 if up else -2, 0), device_id_type=MESH)

    def arrive(turn, k, h, slot):
        hop(turn, k, h, slot, targets[0]).wait_recv()

    def pass_on(turn, k):
        arrive(turn, k, 1, pair)
        now = ~early if turn else True
        pl.when(passes & (row == 2) & now)(lambda: passing(turn, k, True).start())
        pl.when(passes & (row == 1) & now)(lambda: passing(turn, k, False).start())

    def pass_late(turn, k):
        pl.when(passes & (row == 2) & early)(lambda: passing(turn, k, True).start())
        pl.when(passes & (row == 1) & early)(lambda: passing(turn, k, False).start())

    wrap = jnp.where(ry == 0, 2, 3)
    beyond = jnp.where(row == 3, 0, 1)
    over = (lax.rem(rx + jnp.where(row == 3, 1, nrx - 1), nrx), nry - 1 - ry, tp)

    def turning(turn, k, h):
        return pltpu.make_async_remote_copy(
            src_ref=near.at[(turn, k, h, wrap) + cut(k)], dst_ref=near.at[(turn, k, h, beyond) + cut(k)],
            send_sem=turn_send.at[turn, k, h], recv_sem=near_recv.at[turn, k, h, beyond],
            device_id=over, device_id_type=MESH)

    bent = {}

    def bend(turn, last, who):
        here = corner & early if who else corner & ~early
        while bent.setdefault((turn, who), 0) <= min(last, CHUNKS - 1):
            k = bent[turn, who]
            bent[turn, who] += 1
            for h in range(2):
                @pl.when(here)
                def _():
                    arrive(turn, k, h, wrap)
                    turning(turn, k, h).start()

    def start(copy):
        copy.start()

    hear(2)
    tell(3)
    for copy in loads:
        copy.wait()

    for k in range(CHUNKS):
        for copy in share_copies[k]:
            copy.wait_recv()
        shares[(k, tp) + cut(k)] = parts[(k, tp) + cut(k)]
        for h in range(2):
            at = piece(k, h)
            gradient = shares[(k, h) + cut(k)].astype(jnp.float32)
            for other_chip in range(1, ntp // 2):
                gradient += shares[(k, 2 * other_chip + h) + cut(k)].astype(jnp.float32)
            first_new = beta_one * one[at] + (1.0 - beta_one) * gradient
            second_new = beta_two * two[at] + (1.0 - beta_two) * gradient * gradient
            one_out[at] = first_new
            two_out[at] = second_new
            adjusted = first_new / first_fix / (jnp.sqrt(second_new / second_fix) + epsilon)
            weight = current[at]
            now = weight - learn_rate * (adjusted + decay_rate * weight)
            current[at] = now
            sent[(0, k, h) + cut(k)] = (now - public[at]).astype(jnp.bfloat16)
            if k:
                each_hop(0, k, h, start)
        each_step(0, k, start)
        if k:
            pass_on(0, k - 1)
        else:
            hear(3)
            for h in range(2):
                each_hop(0, k, h, start)
    pass_on(0, CHUNKS - 1)

    for turn in range(ROUNDS):
        for k in range(CHUNKS):
            bend(turn, k + AHEAD[turn][0] - 1, True)
            bend(turn, k + AHEAD[turn][1] - 1, False)
            for h in range(2):
                at = piece(k, h)
                pl.when(~corner)(functools.partial(arrive, turn, k, h, wrap))
                arrive(turn, k, h, 5 - wrap)
                arrive(turn, k, h, 1 - pair)
                if h == 0:
                    arrive(turn, k, h, pair)
                beside_all = near[(turn, k, h, 0) + cut(k)].astype(jnp.float32)
                for slot in range(1, 4):
                    beside_all += near[(turn, k, h, slot) + cut(k)].astype(jnp.float32)
                own = sent[(turn, k, h) + cut(k)].astype(jnp.float32)
                public_new = public[at] + own
                mixture_new = mixture[at] + (own + beside_all) / 5.0
                now = current[at] + step_size * (mixture_new - public_new)
                if turn == ROUNDS - 1:
                    weight_out[at] = now
                    public_out[at] = public_new
                    mixture_out[at] = mixture_new
                else:
                    current[at] = now
                    public[at] = public_new
                    mixture[at] = mixture_new
                    sent[(turn + 1, k, h) + cut(k)] = (now - public_new).astype(jnp.bfloat16)
                    each_hop(turn + 1, k, h, start)
            if turn < ROUNDS - 1:
                if k:
                    pass_on(turn + 1, k - 1)
                if k >= LAG:
                    bend(turn + 1, k - LAG, True)
                    bend(turn + 1, k - LAG, False)
                each_step(turn + 1, k, start, early)
        if turn < ROUNDS - 1:
            pass_on(turn + 1, CHUNKS - 1)
            for k in range(CHUNKS):
                each_step(turn + 1, k, start, ~early)
                each_far(turn + 1, k, start)
                pass_late(turn + 1, k)

    for copy in act_copies + grad_copies:
        copy.wait_send()
    for copies in share_copies:
        for copy in copies:
            copy.wait_send()
    for turn in range(ROUNDS):
        for k in range(CHUNKS):
            each_step(turn, k, lambda copy: copy.wait_send())
            if turn:
                each_far(turn, k, lambda copy: copy.wait_send())
            for h in range(2):
                each_hop(turn, k, h, lambda copy: copy.wait_send())
                pl.when(corner)(lambda turn=turn, k=k, h=h: turning(turn, k, h).wait_send())
            pl.when(passes)(lambda turn=turn, k=k: passing(turn, k, True).wait_send())


def store(*refs):
    srcs, dsts, sems = refs[:5], refs[5:10], refs[10]
    copies = [pltpu.make_async_copy(src, dst, sems.at[i]) for i, (src, dst) in enumerate(zip(srcs, dsts))]
    for copy in copies:
        copy.start()
    for copy in copies:
        copy.wait()


def per_device(weight, public, mixture, moment_one, moment_two, stored, out_grad):
    rows, width = weight.shape[2:]
    tokens = out_grad.shape[2]
    step = max(WIDTHS)
    assert 2 * sum(WIDTHS) == width
    ntp = lax.axis_size("tp")
    whole = jax.ShapeDtypeStruct((rows, width), jnp.float32)
    held = pltpu.VMEM((rows, width), jnp.float32)
    dma = pltpu.SemaphoreType.DMA
    outs = pl.pallas_call(
        kernel,
        out_shape=[pltpu.VMEM((rows, width), jnp.float32)] * 5,
        in_specs=[pl.BlockSpec(memory_space=pl.ANY)] * 7,
        out_specs=[pl.BlockSpec(memory_space=pltpu.VMEM)] * 5,
        scratch_shapes=[held] * 5 + [
            pltpu.VMEM((ntp, rows, 2 * tokens), jnp.bfloat16),
            pltpu.VMEM((2 * tokens, width // 2), jnp.bfloat16),
            pltpu.VMEM((CHUNKS, ntp, rows, step), jnp.bfloat16),
            pltpu.VMEM((CHUNKS, ntp, rows, step), jnp.bfloat16),
            pltpu.VMEM((ROUNDS, CHUNKS, 2, rows, step), jnp.bfloat16),
            pltpu.VMEM((ROUNDS, CHUNKS, 2, 4, rows, step), jnp.bfloat16),
            dma((7,)), dma((ntp,)), dma((ntp,)), dma((CHUNKS,)), dma((CHUNKS,)),
            dma((CHUNKS, ntp)), dma((CHUNKS, ntp)),
            dma((ROUNDS, CHUNKS, 2, 4)), dma((ROUNDS, CHUNKS, 2, 4)), dma((ROUNDS, CHUNKS)), dma((ROUNDS, CHUNKS, 2)),
            pltpu.SemaphoreType.REGULAR((4,)),
        ],
        name="gossip_step",
        compiler_params=pltpu.CompilerParams(collective_id=0, has_side_effects=True),
    )(*(a[0, 0] for a in (weight, public, mixture, moment_one, moment_two, stored, out_grad)))
    outs = pl.pallas_call(
        store,
        out_shape=[whole] * 5,
        in_specs=[pl.BlockSpec(memory_space=pltpu.VMEM)] * 5,
        out_specs=[pl.BlockSpec(memory_space=pl.ANY)] * 5,
        scratch_shapes=[dma((5,))],
        name="store",
    )(*(pltpu.with_memory_space_constraint(o, pltpu.VMEM) for o in outs))
    return tuple(o[None, None] for o in outs)


def solution(mesh):
    spec = P("rx", "ry", "tp", None)
    return jax.shard_map(
        per_device, mesh=mesh, in_specs=(spec,) * 7, out_specs=(spec,) * 5, check_vma=False
    )
```
